256 devices in a mesh: lat: 16 (over x_lo, y, core), lon: 16 (over x_hi, z).
Axes of the slice: x: 4 (x_hi: 2, x_lo: 2; x = x_hi * 2 + x_lo), y: 4, z: 8, core: 2. Of those that a mesh axis runs over, the one named last changes fastest.
Arguments:
- ocean_state: bfloat16 [77, 512, 2048], P(None, 'lat', 'lon'), may hold values from -6 to 6
- land_sea: int32 [512, 2048], P('lat', 'lon'), may hold values 0 or 1
- stem_weight: bfloat16 [2, 192, 77], replicated, may hold values from -0.625 to 0.625
- down_weight: bfloat16 [2, 384, 192, 2, 2], replicated, may hold values from -0.21875 to 0.21875
- coarse_depthwise: bfloat16 [2, 384, 7, 7], replicated, may hold values from -0.875 to 0.875
- expand_weight: bfloat16 [2, 1536, 384], replicated, may hold values from -0.3125 to 0.3125
- reduce_weight: bfloat16 [2, 384, 1536], replicated, may hold values from -0.15625 to 0.15625
- up_weight: bfloat16 [2, 4, 4, 192, 384], replicated, may hold values from -0.15625 to 0.15625
- fine_depthwise: bfloat16 [2, 192, 7, 7], replicated, may hold values from -0.875 to 0.875
- head_weight: bfloat16 [2, 77, 192], replicated, may hold values from -0.4375 to 0.4375
Outputs:
- next_state: bfloat16 [77, 512, 2048], P(None, 'lat', 'lon')
The draws below stay inside these ranges and needn't reach their ends.
All inputs are finite; a program needn't handle non-finite values. No bound on the sum of `land_sea` on one device may be relied on, other than what follows from the above.
Results may differ from the reference program's by a relative error of at most 0.0065.
Values may be sent and summed in bfloat16 or wider, within the bound.
A program may use at most 128 MiB of HBM per device.

```python
import jax
import jax.numpy as jnp
from jax import lax

STATE = 77
C0 = 192
C1 = 384
HIDDEN_SIZE = 1536
MEMBERS = 2
NLAT = 512
NLON = 2048


def plant(values, rng, least, largest):
    place = [jax.random.randint(jax.random.fold_in(rng, axis), (), 0, length) for axis, length in enumerate(values.shape)]
    longest = values.shape.index(max(values.shape))
    neighbour = place[:longest] + [(place[longest] + 1) % values.shape[longest]] + place[longest + 1:]
    return values.at[tuple(place)].set(least).at[tuple(neighbour)].set(largest)


def steps_of(stream_key, extent, cuts, least, top_value):
    def one(dim, shards_of):
        steps = jax.random.uniform(jax.random.fold_in(jax.random.fold_in(stream_key, 6), dim), (shards_of,), jnp.float32, least / len(cuts), top_value / len(cuts))
        return jnp.repeat(jnp.exp(steps), extent[dim] // shards_of).reshape((-1,) + (1,) * (len(extent) - dim - 1))

    level = one(*cuts[0])
    for cut in cuts[1:]:
        level = level * one(*cut)
    return level


def noise(own_key, dims, width, reach, split=(), kind=jnp.bfloat16):
    values = jax.random.normal(own_key, dims, jnp.float32) * width
    if len(split) > 0:
        values = steps_of(own_key, dims, split, -0.22, 0.18) * values
    return jnp.clip(values, min=-reach, max=reach).astype(kind)


def setup_inputs(seed: int = 0) -> dict:
    arg_keys = jax.random.split(jax.random.key(seed), 11)
    ocean_state = noise(arg_keys[0], (STATE, NLAT, NLON), 1.0, 6.0, ((1, 16), (2, 16)))
    land_sea = plant((jax.random.randint(arg_keys[1], (NLAT, NLON), 0, 4) < 3).astype(jnp.int32), jax.random.fold_in(arg_keys[1], 1), 0, 1)
    stem_weight = noise(arg_keys[2], (MEMBERS, C0, STATE), STATE ** -0.5, 0.625)
    down_weight = noise(arg_keys[3], (MEMBERS, C1, C0, 2, 2), (4 * C0) ** -0.5, 0.21875)
    coarse_depthwise = noise(arg_keys[4], (MEMBERS, C1, 7, 7), 49 ** -0.5, 0.875)
    expand_weight = noise(arg_keys[5], (MEMBERS, HIDDEN_SIZE, C1), C1 ** -0.5, 0.3125)
    reduce_weight = noise(arg_keys[6], (MEMBERS, C1, HIDDEN_SIZE), HIDDEN_SIZE ** -0.5, 0.15625)
    up_weight = noise(arg_keys[7], (MEMBERS, 4, 4, C0, C1), (4 * C1) ** -0.5, 0.15625)
    fine_depthwise = noise(arg_keys[8], (MEMBERS, C0, 7, 7), 49 ** -0.5, 0.875)
    head_weight = noise(arg_keys[9], (MEMBERS, STATE, C0), C0 ** -0.5, 0.4375)
    return {"ocean_state": ocean_state, "land_sea": land_sea, "stem_weight": stem_weight, "down_weight": down_weight, "coarse_depthwise": coarse_depthwise, "expand_weight": expand_weight, "reduce_weight": reduce_weight, "up_weight": up_weight, "fine_depthwise": fine_depthwise, "head_weight": head_weight}


TAP_TABLE = (((1, 1), (3, 0)), ((2, 1), (0, 2)))

def as_float(values):
    return values.astype(jnp.float32)

def extend_field(field_in, margin):
    height = field_in.shape[2]
    south_rows = jnp.zeros(field_in.shape[:2] + (margin, field_in.shape[3]), field_in.dtype)
    north_rows = field_in[:, :, height - margin:, :][:, :, ::-1, ::-1]
    row_ext = jnp.concatenate([south_rows, field_in, north_rows], axis=2)
    return jnp.concatenate([row_ext[:, :, :, row_ext.shape[3] - margin:], row_ext, row_ext[:, :, :, :margin]], axis=3)

def depthwise_sum(extended, kernel, height, breadth):
    widened = extended.astype(jnp.float32)
    kern_float = kernel.astype(jnp.float32)
    summed = jnp.zeros(extended.shape[:2] + (height, breadth), jnp.float32)
    for row_tap in range(7):
        for col_tap in range(7):
            weight_now = kern_float[:, :, row_tap, col_tap][:, :, None, None]
            summed = summed + weight_now * widened[:, :, row_tap:row_tap + height, col_tap:col_tap + breadth]
    return summed

def channel_norm(values):
    average = lax.optimization_barrier(jnp.mean(values, axis=1, keepdims=True))
    centred = values - average
    spread = lax.optimization_barrier(jnp.mean(centred * centred, axis=1, keepdims=True))
    return centred * lax.rsqrt(spread + 1e-06)

def upsample(padded, up_weight, height, breadth):
    parity_rows = []
    for row_par in range(2):
        parity_cols = []
        for col_par in range(2):
            summed = jnp.zeros((padded.shape[0], up_weight.shape[3], height, breadth), jnp.float32)
            for row_tap, row_off in TAP_TABLE[row_par]:
                for col_tap, col_off in TAP_TABLE[col_par]:
                    window = padded[:, :, row_off:row_off + height, col_off:col_off + breadth]
                    summed = summed + jnp.einsum('moi,miab->moab', as_float(up_weight[:, row_tap, col_tap]), as_float(window))
            parity_cols.append(summed)
        parity_rows.append(jnp.stack(parity_cols, axis=-1))
    joined = jnp.stack(parity_rows, axis=3)
    return joined.reshape(joined.shape[0], joined.shape[1], 2 * height, 2 * breadth)

def member_delta(masked, stem_weight, down_weight, coarse_depthwise, expand_weight, reduce_weight, up_weight, fine_depthwise, head_weight):
    features = jnp.einsum('moi,ihw->mohw', as_float(stem_weight), as_float(masked)).astype(jnp.bfloat16)
    mcount, channels, height, breadth = features.shape
    half_rows = height // 2
    half_cols = breadth // 2
    blocks_view = features.reshape(mcount, channels, half_rows, 2, half_cols, 2)
    coarse = jnp.einsum('moipq,miapbq->moab', as_float(down_weight), as_float(blocks_view)).astype(jnp.bfloat16)
    mixed_out = depthwise_sum(extend_field(coarse, 3), coarse_depthwise, half_rows, half_cols)
    normed = channel_norm(mixed_out).astype(jnp.bfloat16)
    hidden = jax.nn.gelu(jnp.einsum('mhc,mcab->mhab', as_float(expand_weight), as_float(normed)), approximate=True).astype(jnp.bfloat16)
    block_out = (as_float(coarse) + jnp.einsum('mch,mhab->mcab', as_float(reduce_weight), as_float(hidden))).astype(jnp.bfloat16)
    lifted = upsample(extend_field(block_out, 1), up_weight, half_rows, half_cols)
    united = (as_float(features) + lifted).astype(jnp.bfloat16)
    smooth = depthwise_sum(extend_field(united, 3), fine_depthwise, height, breadth)
    fine_normed = channel_norm(smooth).astype(jnp.bfloat16)
    return jnp.einsum('mvo,mohw->mvhw', as_float(head_weight), as_float(fine_normed))

def reference(ocean_state, land_sea, stem_weight, down_weight, coarse_depthwise, expand_weight, reduce_weight, up_weight, fine_depthwise, head_weight):
    mask_bf = land_sea.astype(jnp.bfloat16)
    masked = ocean_state * mask_bf[None]
    deltas = []
    for member in range(stem_weight.shape[0]):
        chosen = slice(member, member + 1)
        deltas.append(member_delta(masked, stem_weight[chosen], down_weight[chosen], coarse_depthwise[chosen], expand_weight[chosen], reduce_weight[chosen], up_weight[chosen], fine_depthwise[chosen], head_weight[chosen]))
    mean_delta = lax.optimization_barrier(jnp.mean(jnp.concatenate(deltas, axis=0), axis=0))
    return (as_float(ocean_state) + as_float(land_sea)[None] * mean_delta).astype(jnp.bfloat16)
```

```python
import jax
import jax.numpy as jnp
from jax import lax
from jax.sharding import PartitionSpec as P

TAP_TABLE = (((1, 1), (3, 0)), ((2, 1), (0, 2)))
F32 = jnp.float32
BF16 = jnp.bfloat16


def extend_field(field, width):
    nlat = lax.axis_size("lat")
    nlon = lax.axis_size("lon")
    rows, cols = field.shape[1], field.shape[2]
    west_edge = field[:, :, :width]
    east_edge = field[:, :, cols - width :]
    from_west = lax.ppermute(east_edge, "lon", [(j, (j + 1) % nlon) for j in range(nlon)])
    from_east = lax.ppermute(west_edge, "lon", [(j, (j - 1) % nlon) for j in range(nlon)])
    wide = jnp.concatenate([from_west, field, from_east], axis=2)
    top = wide[:, rows - width :]
    bottom = wide[:, :width]
    south = lax.ppermute(top, "lat", [(i, i + 1) for i in range(nlat - 1)])
    north = lax.ppermute(bottom, "lat", [(i + 1, i) for i in range(nlat - 1)])
    folded = lax.ppermute(top, "lon", [(j, nlon - 1 - j) for j in range(nlon)])[:, ::-1, ::-1]
    at_top = lax.axis_index("lat") == nlat - 1
    north = jnp.where(at_top, folded, north)
    return jnp.concatenate([south, wide, north], axis=1)


def depthwise_sum(extended, kernel, height, breadth):
    widened = extended.astype(F32)
    kern = kernel.astype(F32)
    summed = None
    for row_tap in range(7):
        for col_tap in range(7):
            term = kern[:, None, None, :, row_tap, col_tap] * widened[
                :, row_tap : row_tap + height, col_tap : col_tap + breadth, :
            ]
            summed = term if summed is None else summed + term
    return summed


def channel_norm(values):
    average = jnp.mean(values, axis=-1, keepdims=True)
    centred = values - average
    spread = jnp.mean(centred * centred, axis=-1, keepdims=True)
    return centred * lax.rsqrt(spread + 1e-06)


def per_device(
    ocean_state,
    land_sea,
    stem_weight,
    down_weight,
    coarse_depthwise,
    expand_weight,
    reduce_weight,
    up_weight,
    fine_depthwise,
    head_weight,
):
    masked = ocean_state * land_sea.astype(BF16)[None]
    _, height, breadth = masked.shape
    half_rows, half_cols = height // 2, breadth // 2

    features = {}
    coarse_acc = None
    for p in range(2):
        for q in range(2):
            part = masked[:, p::2, q::2]
            feat = jnp.einsum(
                "moi,iab->mabo", stem_weight, part, preferred_element_type=F32
            ).astype(BF16)
            features[p, q] = feat
            term = jnp.einsum(
                "moi,mabi->mabo", down_weight[:, :, :, p, q], feat, preferred_element_type=F32
            )
            coarse_acc = term if coarse_acc is None else coarse_acc + term
    coarse = coarse_acc.astype(BF16)

    mixed = depthwise_sum(extend_field(coarse, 3), coarse_depthwise, half_rows, half_cols)
    normed = channel_norm(mixed).astype(BF16)
    hidden = jax.nn.gelu(
        jnp.einsum("mhc,mabc->mabh", expand_weight, normed, preferred_element_type=F32),
        approximate=True,
    ).astype(BF16)
    block_out = (
        coarse.astype(F32)
        + jnp.einsum("mch,mabh->mabc", reduce_weight, hidden, preferred_element_type=F32)
    ).astype(BF16)

    padded = extend_field(block_out, 1)
    rows_out = []
    for p in range(2):
        cols_out = []
        for q in range(2):
            lifted = None
            for row_tap, row_off in TAP_TABLE[p]:
                for col_tap, col_off in TAP_TABLE[q]:
                    window = padded[:, row_off : row_off + half_rows, col_off : col_off + half_cols, :]
                    term = jnp.einsum(
                        "moi,mabi->mabo",
                        up_weight[:, row_tap, col_tap],
                        window,
                        preferred_element_type=F32,
                    )
                    lifted = term if lifted is None else lifted + term
            cols_out.append((features[p, q].astype(F32) + lifted).astype(BF16))
        rows_out.append(jnp.stack(cols_out, axis=3))
    joined = jnp.stack(rows_out, axis=2)
    united = joined.reshape(joined.shape[0], height, breadth, joined.shape[-1])

    smooth = depthwise_sum(extend_field(united, 3), fine_depthwise, height, breadth)
    fine_normed = channel_norm(smooth).astype(BF16)
    total = jnp.einsum("mvo,myxo->vyx", head_weight, fine_normed, preferred_element_type=F32)
    mean_delta = total * (1.0 / head_weight.shape[0])
    return (ocean_state.astype(F32) + land_sea.astype(F32)[None] * mean_delta).astype(BF16)


def solution(mesh):
    placed = (P(None, "lat", "lon"), P("lat", "lon"), P(), P(), P(), P(), P(), P(), P(), P())
    return jax.shard_map(
        per_device, mesh=mesh, in_specs=placed, out_specs=P(None, "lat", "lon"), check_vma=False
    )
```

```python
import jax
import jax.numpy as jnp
from jax import lax
from jax.sharding import PartitionSpec as P

TAP_TABLE = (((1, 1), (3, 0)), ((2, 1), (0, 2)))
F32 = jnp.float32
BF16 = jnp.bfloat16


def extend_field(field, width):
    nlat = lax.axis_size("lat")
    nlon = lax.axis_size("lon")
    rows, cols = field.shape[1], field.shape[2]
    west_edge = field[:, :, :width]
    east_edge = field[:, :, cols - width :]
    from_west = lax.ppermute(east_edge, "lon", [(j, (j + 1) % nlon) for j in range(nlon)])
    from_east = lax.ppermute(west_edge, "lon", [(j, (j - 1) % nlon) for j in range(nlon)])
    wide = jnp.concatenate([from_west, field, from_east], axis=2)
    top = wide[:, rows - width :]
    bottom = wide[:, :width]
    south = lax.ppermute(top, "lat", [(i, i + 1) for i in range(nlat - 1)])
    north = lax.ppermute(bottom, "lat", [(i + 1, i) for i in range(nlat - 1)])
    folded = lax.ppermute(top, "lon", [(j, nlon - 1 - j) for j in range(nlon)])[:, ::-1, ::-1]
    at_top = lax.axis_index("lat") == nlat - 1
    north = jnp.where(at_top, folded, north)
    return jnp.concatenate([south, wide, north], axis=1)


def depthwise_sum(extended, kernel, height, breadth):
    channels = extended.shape[-1]
    outs = []
    for member in range(extended.shape[0]):
        taps = jnp.transpose(kernel[member], (1, 2, 0))[:, :, None, :]
        outs.append(
            lax.conv_general_dilated(
                extended[member : member + 1],
                taps,
                (1, 1),
                "VALID",
                dimension_numbers=("NHWC", "HWIO", "NHWC"),
                feature_group_count=channels,
                preferred_element_type=F32,
            )
        )
    return jnp.concatenate(outs, axis=0)


def channel_norm(values):
    average = jnp.mean(values, axis=-1, keepdims=True)
    centred = values - average
    spread = jnp.mean(centred * centred, axis=-1, keepdims=True)
    return centred * lax.rsqrt(spread + 1e-06)


def per_device(
    ocean_state,
    land_sea,
    stem_weight,
    down_weight,
    coarse_depthwise,
    expand_weight,
    reduce_weight,
    up_weight,
    fine_depthwise,
    head_weight,
):
    masked = ocean_state * land_sea.astype(BF16)[None]
    _, height, breadth = masked.shape
    half_rows, half_cols = height // 2, breadth // 2

    full_features = jnp.einsum(
        "moi,iyx->myxo", stem_weight, masked, preferred_element_type=F32
    ).astype(BF16)
    split = full_features.reshape(
        full_features.shape[0], half_rows, 2, half_cols, 2, full_features.shape[-1]
    )
    features = {}
    coarse_acc = None
    for p in range(2):
        for q in range(2):
            feat = split[:, :, p, :, q, :]
            features[p, q] = feat
            term = jnp.einsum(
                "moi,mabi->mabo", down_weight[:, :, :, p, q], feat, preferred_element_type=F32
            )
            coarse_acc = term if coarse_acc is None else coarse_acc + term
    coarse = coarse_acc.astype(BF16)

    mixed = depthwise_sum(extend_field(coarse, 3), coarse_depthwise, half_rows, half_cols)
    normed = channel_norm(mixed).astype(BF16)
    hidden = jax.nn.gelu(
        jnp.einsum("mhc,mabc->mabh", expand_weight, normed, preferred_element_type=F32),
        approximate=True,
    ).astype(BF16)
    block_out = (
        coarse.astype(F32)
        + jnp.einsum("mch,mabh->mabc", reduce_weight, hidden, preferred_element_type=F32)
    ).astype(BF16)

    padded = extend_field(block_out, 1)
    rows_out = []
    for p in range(2):
        cols_out = []
        for q in range(2):
            lifted = None
            for row_tap, row_off in TAP_TABLE[p]:
                for col_tap, col_off in TAP_TABLE[q]:
                    window = padded[:, row_off : row_off + half_rows, col_off : col_off + half_cols, :]
                    term = jnp.einsum(
                        "moi,mabi->mabo",
                        up_weight[:, row_tap, col_tap],
                        window,
                        preferred_element_type=F32,
                    )
                    lifted = term if lifted is None else lifted + term
            cols_out.append((features[p, q].astype(F32) + lifted).astype(BF16))
        rows_out.append(jnp.stack(cols_out, axis=3))
    joined = jnp.stack(rows_out, axis=2)
    united = joined.reshape(joined.shape[0], height, breadth, joined.shape[-1])

    smooth = depthwise_sum(extend_field(united, 3), fine_depthwise, height, breadth)
    fine_normed = channel_norm(smooth).astype(BF16)
    total = jnp.einsum("mvo,myxo->vyx", head_weight, fine_normed, preferred_element_type=F32)
    mean_delta = total * (1.0 / head_weight.shape[0])
    return (ocean_state.astype(F32) + land_sea.astype(F32)[None] * mean_delta).astype(BF16)


def solution(mesh):
    placed = (P(None, "lat", "lon"), P("lat", "lon"), P(), P(), P(), P(), P(), P(), P(), P())
    return jax.shard_map(
        per_device, mesh=mesh, in_specs=placed, out_specs=P(None, "lat", "lon"), check_vma=False
    )
```

```python
import jax
import jax.numpy as jnp
from jax import lax
from jax.sharding import PartitionSpec as P

TAP_TABLE = (((1, 1), (3, 0)), ((2, 1), (0, 2)))
F32 = jnp.float32
BF16 = jnp.bfloat16


def flip_cols(block):
    cols = block.shape[2]
    anti = jnp.eye(cols, dtype=BF16)[::-1]
    flipped = jnp.einsum("zx,mrxc->mrzc", anti, block, preferred_element_type=F32).astype(BF16)
    return flipped[:, ::-1]


def extend_fields(fields, width):
    nlat = lax.axis_size("lat")
    nlon = lax.axis_size("lon")
    rows, cols = fields[0].shape[0], fields[0].shape[1]
    west_edge = jnp.stack([f[:, :width] for f in fields])
    east_edge = jnp.stack([f[:, cols - width :] for f in fields])
    from_west = lax.ppermute(east_edge, "lon", [(j, (j + 1) % nlon) for j in range(nlon)])
    from_east = lax.ppermute(west_edge, "lon", [(j, (j - 1) % nlon) for j in range(nlon)])
    top = jnp.stack(
        [jnp.concatenate([from_west[m, rows - width :], f[rows - width :], from_east[m, rows - width :]], axis=1)
         for m, f in enumerate(fields)]
    )
    bottom = jnp.stack(
        [jnp.concatenate([from_west[m, :width], f[:width], from_east[m, :width]], axis=1)
         for m, f in enumerate(fields)]
    )
    south = lax.ppermute(top, "lat", [(i, i + 1) for i in range(nlat - 1)])
    north = lax.ppermute(bottom, "lat", [(i + 1, i) for i in range(nlat - 1)])
    folded = flip_cols(lax.ppermute(top, "lon", [(j, nlon - 1 - j) for j in range(nlon)]))
    at_top = lax.axis_index("lat") == nlat - 1
    north = jnp.where(at_top, folded, north)
    out = []
    for m, f in enumerate(fields):
        wide = jnp.concatenate([from_west[m], f, from_east[m]], axis=1)
        out.append(jnp.concatenate([south[m], wide, north[m]], axis=0))
    return out


def depthwise_sum(extended, kernel):
    channels = extended.shape[-1]
    taps = jnp.transpose(kernel, (1, 2, 0))[:, :, None, :]
    out = lax.conv_general_dilated(
        extended[None],
        taps,
        (1, 1),
        "VALID",
        dimension_numbers=("NHWC", "HWIO", "NHWC"),
        feature_group_count=channels,
        preferred_element_type=F32,
    )
    return out[0]


def channel_norm(values):
    average = jnp.mean(values, axis=-1, keepdims=True)
    centred = values - average
    spread = jnp.mean(centred * centred, axis=-1, keepdims=True)
    return centred * lax.rsqrt(spread + 1e-06)


def per_device(
    ocean_state,
    land_sea,
    stem_weight,
    down_weight,
    coarse_depthwise,
    expand_weight,
    reduce_weight,
    up_weight,
    fine_depthwise,
    head_weight,
):
    masked = ocean_state * land_sea.astype(BF16)[None]
    _, height, breadth = masked.shape
    half_rows, half_cols = height // 2, breadth // 2
    members = range(stem_weight.shape[0])

    features = []
    coarse = []
    for m in members:
        full = jnp.einsum(
            "oi,iyx->yxo", stem_weight[m], masked, preferred_element_type=F32
        ).astype(BF16)
        split = full.reshape(half_rows, 2, half_cols, 2, full.shape[-1])
        parts = {}
        acc = None
        for p in range(2):
            for q in range(2):
                feat = split[:, p, :, q]
                parts[p, q] = feat
                term = jnp.einsum(
                    "oi,abi->abo", down_weight[m, :, :, p, q], feat, preferred_element_type=F32
                )
                acc = term if acc is None else acc + term
        features.append(parts)
        coarse.append(acc.astype(BF16))

    mixed_ext = extend_fields(coarse, 3)
    block_out = []
    for m in members:
        mixed = depthwise_sum(mixed_ext[m], coarse_depthwise[m])
        normed = channel_norm(mixed).astype(BF16)
        hidden = jax.nn.gelu(
            jnp.einsum("hc,abc->abh", expand_weight[m], normed, preferred_element_type=F32),
            approximate=True,
        ).astype(BF16)
        block_out.append(
            (
                coarse[m].astype(F32)
                + jnp.einsum("ch,abh->abc", reduce_weight[m], hidden, preferred_element_type=F32)
            ).astype(BF16)
        )

    padded = extend_fields(block_out, 1)
    united = []
    for m in members:
        rows_out = []
        for p in range(2):
            cols_out = []
            for q in range(2):
                lifted = None
                for row_tap, row_off in TAP_TABLE[p]:
                    for col_tap, col_off in TAP_TABLE[q]:
                        window = padded[m][row_off : row_off + half_rows, col_off : col_off + half_cols]
                        term = jnp.einsum(
                            "oi,abi->abo",
                            up_weight[m, row_tap, col_tap],
                            window,
                            preferred_element_type=F32,
                        )
                        lifted = term if lifted is None else lifted + term
                cols_out.append((features[m][p, q].astype(F32) + lifted).astype(BF16))
            rows_out.append(jnp.stack(cols_out, axis=2))
        joined = jnp.stack(rows_out, axis=1)
        united.append(joined.reshape(height, breadth, joined.shape[-1]))

    smooth_ext = extend_fields(united, 3)
    total = None
    for m in members:
        smooth = depthwise_sum(smooth_ext[m], fine_depthwise[m])
        fine_normed = channel_norm(smooth).astype(BF16)
        tendency = jnp.einsum("vo,yxo->vyx", head_weight[m], fine_normed, preferred_element_type=F32)
        total = tendency if total is None else total + tendency
    mean_delta = total * (1.0 / stem_weight.shape[0])
    return (ocean_state.astype(F32) + land_sea.astype(F32)[None] * mean_delta).astype(BF16)


def solution(mesh):
    placed = (P(None, "lat", "lon"), P("lat", "lon"), P(), P(), P(), P(), P(), P(), P(), P())
    return jax.shard_map(
        per_device, mesh=mesh, in_specs=placed, out_specs=P(None, "lat", "lon"), check_vma=False
    )
```

```python
import jax
import jax.numpy as jnp
from jax import lax
from jax.sharding import PartitionSpec as P

TAP_TABLE = (((1, 1), (3, 0)), ((2, 1), (0, 2)))
F32 = jnp.float32
BF16 = jnp.bfloat16


def flip_cols(block):
    cols = block.shape[2]
    anti = jnp.eye(cols, dtype=BF16)[::-1]
    flipped = jnp.einsum("zx,mrxc->mrzc", anti, block, preferred_element_type=F32).astype(BF16)
    return flipped[:, ::-1]


def extend_fields(fields, width):
    nlat = lax.axis_size("lat")
    nlon = lax.axis_size("lon")
    rows, cols = fields[0].shape[0], fields[0].shape[1]
    west_edge = jnp.stack([f[:, :width] for f in fields])
    east_edge = jnp.stack([f[:, cols - width :] for f in fields])
    from_west = lax.ppermute(east_edge, "lon", [(j, (j + 1) % nlon) for j in range(nlon)])
    from_east = lax.ppermute(west_edge, "lon", [(j, (j - 1) % nlon) for j in range(nlon)])
    top = jnp.stack(
        [jnp.concatenate([from_west[m, rows - width :], f[rows - width :], from_east[m, rows - width :]], axis=1)
         for m, f in enumerate(fields)]
    )
    bottom = jnp.stack(
        [jnp.concatenate([from_west[m, :width], f[:width], from_east[m, :width]], axis=1)
         for m, f in enumerate(fields)]
    )
    south = lax.ppermute(top, "lat", [(i, i + 1) for i in range(nlat - 1)])
    north = lax.ppermute(bottom, "lat", [(i + 1, i) for i in range(nlat - 1)])
    folded = flip_cols(lax.ppermute(top, "lon", [(j, nlon - 1 - j) for j in range(nlon)]))
    at_top = lax.axis_index("lat") == nlat - 1
    north = jnp.where(at_top, folded, north)
    out = []
    for m, f in enumerate(fields):
        wide = jnp.concatenate([from_west[m], f, from_east[m]], axis=1)
        out.append(jnp.concatenate([south[m], wide, north[m]], axis=0))
    return out


def depthwise_sum(extended, kernel):
    channels = extended.shape[-1]
    taps = jnp.transpose(kernel, (1, 2, 0))[:, :, None, :]
    out = lax.conv_general_dilated(
        extended[None],
        taps,
        (1, 1),
        "VALID",
        dimension_numbers=("NHWC", "HWIO", "NHWC"),
        feature_group_count=channels,
        preferred_element_type=F32,
    )
    return out[0]


def channel_norm(values):
    average = jnp.mean(values, axis=-1, keepdims=True)
    centred = values - average
    spread = jnp.mean(centred * centred, axis=-1, keepdims=True)
    return centred * lax.rsqrt(spread + 1e-06)


def per_device(
    ocean_state,
    land_sea,
    stem_weight,
    down_weight,
    coarse_depthwise,
    expand_weight,
    reduce_weight,
    up_weight,
    fine_depthwise,
    head_weight,
):
    masked = ocean_state * land_sea.astype(BF16)[None]
    _, height, breadth = masked.shape
    half_rows, half_cols = height // 2, breadth // 2
    members = range(stem_weight.shape[0])

    down_by_parity = jnp.transpose(down_weight, (0, 3, 4, 1, 2))
    features = []
    coarse = []
    for m in members:
        full = jnp.einsum(
            "oi,iyx->yxo", stem_weight[m], masked, preferred_element_type=F32
        ).astype(BF16)
        split = full.reshape(half_rows, 2, half_cols, 2, full.shape[-1])
        parts = {}
        acc = None
        for p in range(2):
            for q in range(2):
                feat = split[:, p, :, q]
                parts[p, q] = feat
                term = jnp.einsum(
                    "oi,abi->abo", down_by_parity[m, p, q], feat, preferred_element_type=F32
                )
                acc = term if acc is None else acc + term
        features.append(parts)
        coarse.append(acc.astype(BF16))

    mixed_ext = extend_fields(coarse, 3)
    block_out = []
    for m in members:
        mixed = depthwise_sum(mixed_ext[m], coarse_depthwise[m])
        normed = channel_norm(mixed).astype(BF16)
        hidden = jax.nn.gelu(
            jnp.einsum("hc,abc->abh", expand_weight[m], normed, preferred_element_type=F32),
            approximate=True,
        ).astype(BF16)
        block_out.append(
            (
                coarse[m].astype(F32)
                + jnp.einsum("ch,abh->abc", reduce_weight[m], hidden, preferred_element_type=F32)
            ).astype(BF16)
        )

    padded = extend_fields(block_out, 1)
    united = []
    for m in members:
        rows_out = []
        for p in range(2):
            cols_out = []
            for q in range(2):
                lifted = None
                for row_tap, row_off in TAP_TABLE[p]:
                    for col_tap, col_off in TAP_TABLE[q]:
                        window = padded[m][row_off : row_off + half_rows, col_off : col_off + half_cols]
                        term = jnp.einsum(
                            "oi,abi->abo",
                            up_weight[m, row_tap, col_tap],
                            window,
                            preferred_element_type=F32,
                        )
                        lifted = term if lifted is None else lifted + term
                cols_out.append((features[m][p, q].astype(F32) + lifted).astype(BF16))
            rows_out.append(jnp.stack(cols_out, axis=2))
        joined = jnp.stack(rows_out, axis=1)
        united.append(joined.reshape(height, breadth, joined.shape[-1]))

    smooth_ext = extend_fields(united, 3)
    total = None
    for m in members:
        smooth = depthwise_sum(smooth_ext[m], fine_depthwise[m])
        fine_normed = channel_norm(smooth).astype(BF16)
        tendency = jnp.einsum("vo,yxo->vyx", head_weight[m], fine_normed, preferred_element_type=F32)
        total = tendency if total is None else total + tendency
    mean_delta = total * (1.0 / stem_weight.shape[0])
    return (ocean_state.astype(F32) + land_sea.astype(F32)[None] * mean_delta).astype(BF16)


def solution(mesh):
    placed = (P(None, "lat", "lon"), P("lat", "lon"), P(), P(), P(), P(), P(), P(), P(), P())
    return jax.shard_map(
        per_device, mesh=mesh, in_specs=placed, out_specs=P(None, "lat", "lon"), check_vma=False
    )
```

```python
import jax
import jax.numpy as jnp
from jax import lax
from jax.sharding import PartitionSpec as P

TAP_TABLE = (((1, 1), (3, 0)), ((2, 1), (0, 2)))
F32 = jnp.float32
BF16 = jnp.bfloat16


def flip_cols(block):
    cols = block.shape[2]
    anti = jnp.eye(cols, dtype=BF16)[::-1]
    flipped = jnp.einsum("zx,mrxc->mrzc", anti, block, preferred_element_type=F32).astype(BF16)
    return flipped[:, ::-1]


def extend_fields(fields, width):
    nlat = lax.axis_size("lat")
    nlon = lax.axis_size("lon")
    rows, cols = fields[0].shape[0], fields[0].shape[1]
    west_edge = jnp.stack([f[:, :width] for f in fields])
    east_edge = jnp.stack([f[:, cols - width :] for f in fields])
    from_west = lax.ppermute(east_edge, "lon", [(j, (j + 1) % nlon) for j in range(nlon)])
    from_east = lax.ppermute(west_edge, "lon", [(j, (j - 1) % nlon) for j in range(nlon)])
    top = jnp.stack(
        [jnp.concatenate([from_west[m, rows - width :], f[rows - width :], from_east[m, rows - width :]], axis=1)
         for m, f in enumerate(fields)]
    )
    bottom = jnp.stack(
        [jnp.concatenate([from_west[m, :width], f[:width], from_east[m, :width]], axis=1)
         for m, f in enumerate(fields)]
    )
    south = lax.ppermute(top, "lat", [(i, i + 1) for i in range(nlat - 1)])
    north = lax.ppermute(bottom, "lat", [(i + 1, i) for i in range(nlat - 1)])
    folded = flip_cols(lax.ppermute(top, "lon", [(j, nlon - 1 - j) for j in range(nlon)]))
    at_top = lax.axis_index("lat") == nlat - 1
    north = jnp.where(at_top, folded, north)
    out = []
    for m, f in enumerate(fields):
        wide = jnp.concatenate([from_west[m], f, from_east[m]], axis=1)
        out.append(jnp.concatenate([south[m], wide, north[m]], axis=0))
    return out


def depthwise_sum(extended, kernel):
    channels = extended.shape[-1]
    taps = jnp.transpose(kernel, (1, 2, 0))[:, :, None, :]
    out = lax.conv_general_dilated(
        extended[None],
        taps,
        (1, 1),
        "VALID",
        dimension_numbers=("NHWC", "HWIO", "NHWC"),
        feature_group_count=channels,
        preferred_element_type=F32,
    )
    return out[0]


def channel_norm(values):
    average = jnp.mean(values, axis=-1, keepdims=True)
    centred = values - average
    spread = jnp.mean(centred * centred, axis=-1, keepdims=True)
    return centred * lax.rsqrt(spread + 1e-06)


def per_device(
    ocean_state,
    land_sea,
    stem_weight,
    down_weight,
    coarse_depthwise,
    expand_weight,
    reduce_weight,
    up_weight,
    fine_depthwise,
    head_weight,
):
    masked = ocean_state * land_sea.astype(BF16)[None]
    _, height, breadth = masked.shape
    half_rows, half_cols = height // 2, breadth // 2
    members = range(stem_weight.shape[0])

    masked_cl = jnp.transpose(masked, (1, 2, 0)).reshape(half_rows, 2, half_cols, 2, masked.shape[0])
    masked_parts = {(p, q): masked_cl[:, p, :, q] for p in range(2) for q in range(2)}
    features = []
    coarse = []
    for m in members:
        parts = {}
        acc = None
        for p in range(2):
            for q in range(2):
                feat = jnp.einsum(
                    "oi,abi->abo", stem_weight[m], masked_parts[p, q], preferred_element_type=F32
                ).astype(BF16)
                parts[p, q] = feat
                term = jnp.einsum(
                    "oi,abi->abo", down_weight[m, :, :, p, q], feat, preferred_element_type=F32
                )
                acc = term if acc is None else acc + term
        features.append(parts)
        coarse.append(acc.astype(BF16))

    mixed_ext = extend_fields(coarse, 3)
    block_out = []
    for m in members:
        mixed = depthwise_sum(mixed_ext[m], coarse_depthwise[m])
        normed = channel_norm(mixed).astype(BF16)
        hidden = jax.nn.gelu(
            jnp.einsum("hc,abc->abh", expand_weight[m], normed, preferred_element_type=F32),
            approximate=True,
        ).astype(BF16)
        block_out.append(
            (
                coarse[m].astype(F32)
                + jnp.einsum("ch,abh->abc", reduce_weight[m], hidden, preferred_element_type=F32)
            ).astype(BF16)
        )

    padded = extend_fields(block_out, 1)
    united = []
    for m in members:
        rows_out = []
        for p in range(2):
            cols_out = []
            for q in range(2):
                lifted = None
                for row_tap, row_off in TAP_TABLE[p]:
                    for col_tap, col_off in TAP_TABLE[q]:
                        window = padded[m][row_off : row_off + half_rows, col_off : col_off + half_cols]
                        term = jnp.einsum(
                            "oi,abi->abo",
                            up_weight[m, row_tap, col_tap],
                            window,
                            preferred_element_type=F32,
                        )
                        lifted = term if lifted is None else lifted + term
                cols_out.append((features[m][p, q].astype(F32) + lifted).astype(BF16))
            rows_out.append(jnp.stack(cols_out, axis=2))
        joined = jnp.stack(rows_out, axis=1)
        united.append(joined.reshape(height, breadth, joined.shape[-1]))

    smooth_ext = extend_fields(united, 3)
    total = None
    for m in members:
        smooth = depthwise_sum(smooth_ext[m], fine_depthwise[m])
        fine_normed = channel_norm(smooth).astype(BF16)
        tendency = jnp.einsum("vo,yxo->vyx", head_weight[m], fine_normed, preferred_element_type=F32)
        total = tendency if total is None else total + tendency
    mean_delta = total * (1.0 / stem_weight.shape[0])
    return (ocean_state.astype(F32) + land_sea.astype(F32)[None] * mean_delta).astype(BF16)


def solution(mesh):
    placed = (P(None, "lat", "lon"), P("lat", "lon"), P(), P(), P(), P(), P(), P(), P(), P())
    return jax.shard_map(
        per_device, mesh=mesh, in_specs=placed, out_specs=P(None, "lat", "lon"), check_vma=False
    )
```

```python
import jax
import jax.numpy as jnp
from jax import lax
from jax.sharding import PartitionSpec as P

TAP_TABLE = (((1, 1), (3, 0)), ((2, 1), (0, 2)))
F32 = jnp.float32
BF16 = jnp.bfloat16


def flip_cols(block):
    cols = block.shape[2]
    anti = jnp.eye(cols, dtype=BF16)[::-1]
    flipped = jnp.einsum("zx,mrxc->mrzc", anti, block, preferred_element_type=F32).astype(BF16)
    return flipped[:, ::-1]


def extend_fields(fields, width):
    nlat = lax.axis_size("lat")
    nlon = lax.axis_size("lon")
    rows, cols = fields[0].shape[0], fields[0].shape[1]
    west_edge = jnp.stack([f[:, :width] for f in fields])
    east_edge = jnp.stack([f[:, cols - width :] for f in fields])
    from_west = lax.ppermute(east_edge, "lon", [(j, (j + 1) % nlon) for j in range(nlon)])
    from_east = lax.ppermute(west_edge, "lon", [(j, (j - 1) % nlon) for j in range(nlon)])
    top = jnp.stack(
        [jnp.concatenate([from_west[m, rows - width :], f[rows - width :], from_east[m, rows - width :]], axis=1)
         for m, f in enumerate(fields)]
    )
    bottom = jnp.stack(
        [jnp.concatenate([from_west[m, :width], f[:width], from_east[m, :width]], axis=1)
         for m, f in enumerate(fields)]
    )
    south = lax.ppermute(top, "lat", [(i, i + 1) for i in range(nlat - 1)])
    north = lax.ppermute(bottom, "lat", [(i + 1, i) for i in range(nlat - 1)])
    fold_pairs = [((nlat - 1) * nlon + j, (nlat - 1) * nlon + nlon - 1 - j) for j in range(nlon)]
    folded = flip_cols(lax.ppermute(top, ("lat", "lon"), fold_pairs))
    at_top = lax.axis_index("lat") == nlat - 1
    north = jnp.where(at_top, folded, north)
    out = []
    for m, f in enumerate(fields):
        wide = jnp.concatenate([from_west[m], f, from_east[m]], axis=1)
        out.append(jnp.concatenate([south[m], wide, north[m]], axis=0))
    return out


def depthwise_sum(extended, kernel):
    channels = extended.shape[-1]
    taps = jnp.transpose(kernel, (1, 2, 0))[:, :, None, :]
    out = lax.conv_general_dilated(
        extended[None],
        taps,
        (1, 1),
        "VALID",
        dimension_numbers=("NHWC", "HWIO", "NHWC"),
        feature_group_count=channels,
        preferred_element_type=F32,
    )
    return out[0]


def channel_norm(values):
    average = jnp.mean(values, axis=-1, keepdims=True)
    centred = values - average
    spread = jnp.mean(centred * centred, axis=-1, keepdims=True)
    return centred * lax.rsqrt(spread + 1e-06)


def per_device(
    ocean_state,
    land_sea,
    stem_weight,
    down_weight,
    coarse_depthwise,
    expand_weight,
    reduce_weight,
    up_weight,
    fine_depthwise,
    head_weight,
):
    masked = ocean_state * land_sea.astype(BF16)[None]
    _, height, breadth = masked.shape
    half_rows, half_cols = height // 2, breadth // 2
    members = range(stem_weight.shape[0])

    masked_cl = jnp.transpose(masked, (1, 2, 0)).reshape(half_rows, 2, half_cols, 2, masked.shape[0])
    masked_parts = {(p, q): masked_cl[:, p, :, q] for p in range(2) for q in range(2)}
    features = []
    coarse = []
    for m in members:
        parts = {}
        acc = None
        for p in range(2):
            for q in range(2):
                feat = jnp.einsum(
                    "oi,abi->abo", stem_weight[m], masked_parts[p, q], preferred_element_type=F32
                ).astype(BF16)
                parts[p, q] = feat
                term = jnp.einsum(
                    "oi,abi->abo", down_weight[m, :, :, p, q], feat, preferred_element_type=F32
                )
                acc = term if acc is None else acc + term
        features.append(parts)
        coarse.append(acc.astype(BF16))

    mixed_ext = extend_fields(coarse, 3)
    block_out = []
    for m in members:
        mixed = depthwise_sum(mixed_ext[m], coarse_depthwise[m])
        normed = channel_norm(mixed).astype(BF16)
        hidden = jax.nn.gelu(
            jnp.einsum("hc,abc->abh", expand_weight[m], normed, preferred_element_type=F32),
            approximate=True,
        ).astype(BF16)
        block_out.append(
            (
                coarse[m].astype(F32)
                + jnp.einsum("ch,abh->abc", reduce_weight[m], hidden, preferred_element_type=F32)
            ).astype(BF16)
        )

    padded = extend_fields(block_out, 1)
    united = []
    for m in members:
        rows_out = []
        for p in range(2):
            cols_out = []
            for q in range(2):
                lifted = None
                for row_tap, row_off in TAP_TABLE[p]:
                    for col_tap, col_off in TAP_TABLE[q]:
                        window = padded[m][row_off : row_off + half_rows, col_off : col_off + half_cols]
                        term = jnp.einsum(
                            "oi,abi->abo",
                            up_weight[m, row_tap, col_tap],
                            window,
                            preferred_element_type=F32,
                        )
                        lifted = term if lifted is None else lifted + term
                cols_out.append((features[m][p, q].astype(F32) + lifted).astype(BF16))
            rows_out.append(jnp.stack(cols_out, axis=2))
        joined = jnp.stack(rows_out, axis=1)
        united.append(joined.reshape(height, breadth, joined.shape[-1]))

    smooth_ext = extend_fields(united, 3)
    total = None
    for m in members:
        smooth = depthwise_sum(smooth_ext[m], fine_depthwise[m])
        fine_normed = channel_norm(smooth).astype(BF16)
        tendency = jnp.einsum("vo,yxo->vyx", head_weight[m], fine_normed, preferred_element_type=F32)
        total = tendency if total is None else total + tendency
    mean_delta = total * (1.0 / stem_weight.shape[0])
    return (ocean_state.astype(F32) + land_sea.astype(F32)[None] * mean_delta).astype(BF16)


def solution(mesh):
    placed = (P(None, "lat", "lon"), P("lat", "lon"), P(), P(), P(), P(), P(), P(), P(), P())
    return jax.shard_map(
        per_device, mesh=mesh, in_specs=placed, out_specs=P(None, "lat", "lon"), check_vma=False
    )
```
